32 devices in a mesh: wide: 16 (over z, x, core), narrow: 2 (over y).
Axes of the slice: x: 2, y: 2, z: 4, core: 2. Of those that a mesh axis runs over, the one named last changes fastest.
Arguments:
- hess_inverse: bfloat16 [26880, 26880], P('wide', 'narrow'), may hold values from -0.0390625 to 0.0390625
- observations: bfloat16 [16, 26880], P('wide', 'narrow'), may hold values from -6 to 6
- adjoint_maps: bfloat16 [210, 2, 6144, 128], P('narrow', None, 'wide'), may hold values from -0.375 to 0.375
Outputs:
- estimate: float32 [6144, 210, 16], P(('wide', 'narrow'))
The draws below stay inside these ranges and needn't reach their ends.
All inputs are finite; a program needn't handle non-finite values.
Results may differ from the reference program's by a relative error of at most 0.004.
Values may be sent and summed in bfloat16 or wider, within the bound.
A program may use at most 128 MiB of HBM per device.

```python
import math
import jax
import jax.numpy as jnp
from jax import lax

S = 128
NT = 210
NF = 210
P_SIZE = 6144
SCEN = 16
NDATA = 26880


def block_levels(own_key, shape, pieces, smallest, high):
    level = 1.0
    for axis_at, parts in pieces:
        steps = jax.random.uniform(jax.random.fold_in(jax.random.fold_in(own_key, 6), axis_at), (parts,), jnp.float32, smallest / len(pieces), high / len(pieces))
        level = level * jnp.repeat(jnp.exp(steps), shape[axis_at] // parts).reshape((-1,) + (1,) * (len(shape) - 1 - axis_at))
    return level


def noise(stream_key, dims, scale, reach, split=(), held_as=jnp.bfloat16):
    values = scale * jax.random.normal(stream_key, dims, jnp.float32)
    if split:
        values = values * block_levels(stream_key, dims, split, -0.22, 0.18)
    return jnp.clip(values, -reach, reach).astype(held_as)


def setup_inputs(seed: int = 0) -> dict:
    key_list = jax.random.split(jax.random.key(seed), 4)
    hess_inverse = noise(key_list[0], (NDATA, NDATA), NDATA ** -0.5, 0.0390625, ((0, 16), (1, 2)))
    observations = noise(key_list[1], (SCEN, NDATA), 1.0, 6.0, ((0, 16), (1, 2)))
    adjoint_maps = noise(key_list[2], (NF, 2, P_SIZE, S), (2 * S * NT // NF) ** -0.5, 0.375, ((0, 2), (2, 16)))
    return dict(hess_inverse=hess_inverse, observations=observations, adjoint_maps=adjoint_maps)


full_turn = 2.0 * math.pi


def analysis_table():
    times_axis = jnp.arange(NT).astype(jnp.float32)
    freqs = jnp.arange(NF).astype(jnp.float32)
    angles = full_turn * times_axis[:, None] * freqs[None, :] / (2.0 * NF)
    return jnp.stack([jnp.cos(angles), -jnp.sin(angles)], axis=-1)


def synthesis_table():
    times_axis = jnp.arange(NT).astype(jnp.float32)
    freqs = jnp.arange(NF).astype(jnp.float32)
    angles = full_turn * freqs[:, None] * times_axis[None, :] / (2.0 * NF)
    return jnp.stack([jnp.cos(angles), -jnp.sin(angles)], axis=1)


def reference(hess_inverse, observations, adjoint_maps):
    highest = lax.Precision.HIGHEST
    observed = observations.astype(jnp.float32)
    block_rows = NDATA // 16
    blocks = hess_inverse.reshape(16, block_rows, NDATA)

    def apply_block(rows_block):
        return jnp.dot(observed, rows_block.astype(jnp.float32).T, precision=highest)

    products = lax.map(apply_block, blocks)
    series = jnp.transpose(products, (1, 0, 2)).reshape(SCEN, NDATA)
    values = series.reshape(SCEN, S, NT)
    spectra = jnp.einsum("nst,tfc->fcsn", values, analysis_table(), precision=highest).astype(jnp.bfloat16)
    spec = spectra.astype(jnp.float32)
    basis = synthesis_table()
    block_count = 8 if P_SIZE % 8 == 0 else 1
    param_block = P_SIZE // block_count
    map_blocks = jnp.transpose(adjoint_maps.reshape(NF, 2, block_count, param_block, S), (2, 0, 1, 3, 4))

    def block_estimate(maps):
        mapped = maps.astype(jnp.float32)
        real_part = jnp.einsum("fps,fsn->fpn", mapped[:, 0], spec[:, 0], precision=highest) - jnp.einsum("fps,fsn->fpn", mapped[:, 1], spec[:, 1], precision=highest)
        imag_part = jnp.einsum("fps,fsn->fpn", mapped[:, 0], spec[:, 1], precision=highest) + jnp.einsum("fps,fsn->fpn", mapped[:, 1], spec[:, 0], precision=highest)
        real_part = lax.optimization_barrier(real_part.astype(jnp.bfloat16)).astype(jnp.float32)
        imag_part = lax.optimization_barrier(imag_part.astype(jnp.bfloat16)).astype(jnp.float32)
        result = jnp.einsum("fpn,ft->ptn", real_part, basis[:, 0], precision=highest) + jnp.einsum("fpn,ft->ptn", imag_part, basis[:, 1], precision=highest)
        return result * (1.0 / NF)

    estimates = lax.map(block_estimate, map_blocks)
    return estimates.reshape(P_SIZE, NT, SCEN)
```

```python
import functools
import math

import jax
import jax.numpy as jnp
import numpy as np
from jax import lax
from jax.experimental import pallas as pl
from jax.experimental.pallas import tpu as pltpu
from jax.sharding import PartitionSpec as P

MESH = pl.DeviceIdType.MESH
LANES = 128


def angles(freqs, times, turn):
    return 2.0 * math.pi * ((freqs * times) % turn) / turn


def analysis_table(nt, nf):
    a = angles(np.arange(nt)[:, None], np.arange(nf)[None, :], 2 * nf)
    return np.stack([np.cos(a), -np.sin(a)], axis=1).astype(np.float32)


def synthesis_table(nt, nf):
    a = angles(np.arange(nf)[:, None], np.arange(nt)[None, :], 2 * nf)
    return np.stack([np.cos(a), -np.sin(a)], axis=1).astype(np.float32)


def gather_kernel(zs, x_ref, out_ref, send, recv):
    w = lax.axis_index("wide")
    z, x, c = w // 4, (w // 2) % 2, w % 2

    def at(zz, xx, cc):
        return (zz * 2 + xx) * 2 + cc

    peers = [at((z + d) % zs, x, c) for d in range(1, zs)] + [at(z, 1 - x, c), at(z, x, 1 - c)]
    barrier = pltpu.get_barrier_semaphore()
    for p in peers:
        pl.semaphore_signal(barrier, inc=1, device_id={"wide": p}, device_id_type=MESH)
    pl.semaphore_wait(barrier, len(peers))

    copies = []

    def put(src, slot, k, target):
        cp = pltpu.make_async_remote_copy(
            src_ref=src, dst_ref=out_ref.at[slot], send_sem=send.at[k], recv_sem=recv.at[k],
            device_id={"wide": target}, device_id_type=MESH)
        cp.start()
        copies.append(cp)
        return cp

    along_z = [put(x_ref, w, d - 1, at((z + d) % zs, x, c)) for d in range(1, zs)]
    base_x = zs - 1
    base_c = base_x + zs
    along_x = [put(x_ref, w, base_x, at(z, 1 - x, c))]
    along_c = [put(x_ref, w, base_c, at(z, x, 1 - c))]
    out_ref[w] = x_ref[...]
    for d in range(1, zs):
        along_z[d - 1].wait_recv()
        slot = at((z + zs - d) % zs, x, c)
        along_x.append(put(out_ref.at[slot], slot, base_x + d, at(z, 1 - x, c)))
        along_c.append(put(out_ref.at[slot], slot, base_c + d, at(z, x, 1 - c)))
    for d in range(zs):
        along_x[d].wait_recv()
        slot = at((z + zs - d) % zs, 1 - x, c)
        along_c.append(put(out_ref.at[slot], slot, base_c + zs + d, at(z, x, 1 - c)))
    for cp in along_c:
        cp.wait_recv()
    for cp in copies:
        cp.wait_send()


def gather_wide(block, wide, ident):
    zs = wide // 4
    n = zs - 1 + zs + 2 * zs
    vm = pl.BlockSpec(memory_space=pltpu.VMEM)
    return pl.pallas_call(
        functools.partial(gather_kernel, zs),
        out_shape=jax.ShapeDtypeStruct((wide,) + block.shape, block.dtype),
        in_specs=[vm], out_specs=vm,
        scratch_shapes=[pltpu.SemaphoreType.DMA((n,)), pltpu.SemaphoreType.DMA((n,))],
        compiler_params=pltpu.CompilerParams(collective_id=ident, has_side_effects=True),
        name=f"gather{ident}",
    )(block)


def map_kernel(fs, groups, half, x_ref, a_hbm, out_ref, a, m32, sent, load, send, recv):
    k = lax.axis_index("narrow")
    other = 1 - k

    def fetch(g, side, h):
        rows = pl.ds(pl.multiple_of(h * half, 64), half)
        return pltpu.make_async_copy(
            a_hbm.at[pl.ds(g * fs, fs), :, rows], a.at[pl.ds(g * fs, fs), :, rows], load.at[side, g])

    for g in range(groups):
        fetch(g, 0, other).start()
    for g in range(groups):
        fetch(g, 1, k).start()

    barrier = pltpu.get_barrier_semaphore()
    pl.semaphore_signal(barrier, inc=1, device_id={"narrow": other}, device_id_type=MESH)
    pl.semaphore_wait(barrier, 1)

    m32[...] = jnp.zeros_like(m32)
    lane = lax.broadcasted_iota(jnp.int32, (8, LANES), 1)

    def chunk(g, h, dst):
        p0 = pl.multiple_of(h * half, 64)
        for i in range(fs):
            f = g * fs + i
            parts = []
            for c in range(2):
                head = a[f, c, pl.ds(p0, 128), :]
                tail = a[f, c, pl.ds(p0 + 128, 64), :]
                parts.append(jnp.concatenate([head, tail, tail], axis=0))
            got = lax.dot_general(
                x_ref[f], jnp.concatenate(parts, axis=1), (((1,), (1,)), ((), ())),
                preferred_element_type=jnp.float32)
            for c in range(2):
                low, high = got[c * 16:c * 16 + 8], got[c * 16 + 8:c * 16 + 16]
                rows = pl.ds(c * 16 + i, 8, stride=32)
                m32[0, rows, :] = low[:, :LANES]
                m32[1, rows, :] = high[:, :LANES]
                m32[2, rows, :] = jnp.where(lane < 64, low[:, LANES:], high[:, LANES:])
        for b in range(3):
            dst[:, :, b * LANES:(b + 1) * LANES] = m32[b].reshape(8, 32, LANES).astype(jnp.bfloat16)

    def across(g):
        return pltpu.make_async_remote_copy(
            src_ref=sent.at[g], dst_ref=out_ref.at[k, g], send_sem=send.at[g], recv_sem=recv.at[g],
            device_id={"narrow": other}, device_id_type=MESH)

    def first(g, _):
        fetch(g, 0, other).wait()
        chunk(g, other, sent.at[g])

        @pl.when(g > 0)
        def _():
            across(g - 1).start()
        return 0

    lax.fori_loop(0, groups, first, 0)

    def second(g, _):
        fetch(g, 1, k).wait()
        chunk(g, k, out_ref.at[k, g])

        @pl.when(g == 0)
        def _():
            across(groups - 1).start()
        return 0

    lax.fori_loop(0, groups, second, 0)

    def drain(g, _):
        across(g).wait()
        return 0

    lax.fori_loop(0, groups, drain, 0)


def apply_maps(x, maps, fs, ident):
    nf, _, points, sensors = maps.shape
    groups, half = nf // fs, points // 2
    vm = pl.BlockSpec(memory_space=pltpu.VMEM)
    return pl.pallas_call(
        functools.partial(map_kernel, fs, groups, half),
        out_shape=jax.ShapeDtypeStruct((2, groups, 8, 32, 2 * half), jnp.bfloat16),
        in_specs=[vm, pl.BlockSpec(memory_space=pltpu.HBM)], out_specs=vm,
        scratch_shapes=[
            pltpu.VMEM(maps.shape, jnp.bfloat16),
            pltpu.VMEM((3, 8 * 32, LANES), jnp.float32),
            pltpu.VMEM((groups, 8, 32, 2 * half), jnp.bfloat16),
            pltpu.SemaphoreType.DMA((2, groups)),
            pltpu.SemaphoreType.DMA((groups,)),
            pltpu.SemaphoreType.DMA((groups,)),
        ],
        compiler_params=pltpu.CompilerParams(
            collective_id=ident, has_side_effects=True, vmem_limit_bytes=48 << 20),
        name="maps",
    )(x, maps)


def time_kernel(scale, m_ref, hi_ref, lo_ref, out_ref):
    blocks, nt = m_ref.shape[0], out_ref.shape[2]
    for j in range(8):
        m = m_ref[:, j].reshape(blocks * 32, m_ref.shape[3])
        got = lax.dot_general(m, hi_ref[...], (((0,), (0,)), ((), ())), preferred_element_type=jnp.float32)
        got += lax.dot_general(m, lo_ref[...], (((0,), (0,)), ((), ())), preferred_element_type=jnp.float32)
        got = (got * scale)[:, :nt]
        out_ref[0:128, j, :] = got[0:128]
        out_ref[0:128, j + 8, :] = got[128:256]
        out_ref[128:192, j, :] = got[256:320]
        out_ref[128:192, j + 8, :] = got[320:384]


def to_time(m, nt, nf, fs):
    blocks = m.shape[0] * m.shape[1]
    table = synthesis_table(nt, nf)
    laid = np.zeros((blocks, 2, 16, 256), np.float32)
    laid[:, :, :fs, :nt] = table.reshape(blocks, fs, 2, nt).transpose(0, 2, 1, 3)
    laid = laid.reshape(blocks * 32, 256)
    hi = laid.astype(jnp.bfloat16)
    lo = (laid - hi.astype(np.float32)).astype(jnp.bfloat16)
    vm = pl.BlockSpec(memory_space=pltpu.VMEM)
    return pl.pallas_call(
        functools.partial(time_kernel, 1.0 / nf),
        out_shape=jax.ShapeDtypeStruct((m.shape[4] // 2, 16, nt), jnp.float32),
        in_specs=[vm] * 3, out_specs=vm,
        compiler_params=pltpu.CompilerParams(vmem_limit_bytes=32 << 20),
        name="time",
    )(m.reshape((blocks,) + m.shape[2:]), jnp.asarray(hi), jnp.asarray(lo))


def per_device(wide, narrow, hess_inverse, observations, adjoint_maps):
    highest = lax.Precision.HIGHEST
    nf_dev, _, points, sensors = adjoint_maps.shape
    nf = nf_dev * narrow
    rows, cols = hess_inverse.shape
    nt = rows * wide // sensors
    scen = observations.shape[0] * wide
    sensors_dev = rows // nt
    fs = max([d for d in range(1, 17) if nf_dev % d == 0])
    tuned = (narrow == 2 and wide == 16 and scen == 16 and sensors == 128 and points == 384
             and cols % LANES == 0 and observations.shape[0] == 1)
    if tuned:
        observed = gather_wide(observations.reshape(cols // LANES, LANES), wide, 0).reshape(scen, cols)
    else:
        observed = lax.all_gather(observations, "wide", axis=0, tiled=True)
    partial_value = lax.dot_general(
        observed, hess_inverse, (((1,), (1,)), ((), ())), preferred_element_type=jnp.float32)
    values = partial_value.reshape(scen, sensors_dev, nt)
    table = jnp.asarray(analysis_table(nt, nf))
    if not tuned:
        terms = jnp.einsum("nst,tcf->sfcn", values, table, precision=highest)
        spectra = lax.psum_scatter(terms, "narrow", scatter_dimension=1, tiled=True).astype(jnp.bfloat16)
        portion = lax.all_gather(spectra, "wide", axis=0, tiled=True)
        both = portion.transpose(1, 2, 3, 0)
        re, im = both[:, 0], both[:, 1]
        x = jnp.concatenate([jnp.concatenate([re, -im], 2), jnp.concatenate([im, re], 2)], 1)
        a = adjoint_maps.transpose(0, 2, 1, 3).reshape(nf_dev, points, 2 * sensors)
        m = jnp.einsum("frk,fpk->frp", x, a, preferred_element_type=jnp.float32).astype(jnp.bfloat16)
        m = m.reshape(nf_dev, 2, scen, points)
        m = lax.all_to_all(m, "narrow", split_axis=3, concat_axis=0, tiled=True)
        est = jnp.einsum("fcnp,fct->ptn", m.astype(jnp.float32), jnp.asarray(synthesis_table(nt, nf)),
                         precision=highest)
        return est * (1.0 / nf)
    terms = jnp.einsum("nst,tcf->scnf", values, table, precision=highest)
    k = lax.axis_index("narrow")
    mine = lax.dynamic_slice_in_dim(terms, k * nf_dev, nf_dev, 3)
    theirs = lax.dynamic_slice_in_dim(terms, (1 - k) * nf_dev, nf_dev, 3)
    came = lax.ppermute(theirs.reshape(-1, nf_dev), "narrow", [(0, 1), (1, 0)])
    spectra = (mine.reshape(-1, nf_dev) + came).astype(jnp.bfloat16)
    full = gather_wide(spectra, wide, 1).reshape(sensors, 2, scen, nf_dev)
    both = full.transpose(3, 1, 2, 0)
    re, im = both[:, 0], both[:, 1]
    x = jnp.concatenate([jnp.concatenate([re, -im], 2), jnp.concatenate([im, re], 2)], 1)
    m = apply_maps(x, adjoint_maps, fs, 2)
    return to_time(m, nt, nf, fs).transpose(0, 2, 1)


def solution(mesh):
    wide, narrow = mesh.shape["wide"], mesh.shape["narrow"]
    return jax.shard_map(
        functools.partial(per_device, wide, narrow),
        mesh=mesh,
        in_specs=(P("wide", "narrow"), P("wide", "narrow"), P("narrow", None, "wide", None)),
        out_specs=P(("wide", "narrow"), None, None),
        check_vma=False,
    )
```

```python
import functools
import math

import jax
import jax.numpy as jnp
import numpy as np
from jax import lax
from jax.experimental import pallas as pl
from jax.experimental.pallas import tpu as pltpu
from jax.sharding import PartitionSpec as P

MESH = pl.DeviceIdType.MESH
LANES = 128


def angles(freqs, times, turn):
    return 2.0 * math.pi * ((freqs * times) % turn) / turn


def analysis_table(nt, nf):
    a = angles(np.arange(nt)[:, None], np.arange(nf)[None, :], 2 * nf)
    return np.stack([np.cos(a), -np.sin(a)], axis=1).astype(np.float32)


def synthesis_table(nt, nf):
    a = angles(np.arange(nf)[:, None], np.arange(nt)[None, :], 2 * nf)
    return np.stack([np.cos(a), -np.sin(a)], axis=1).astype(np.float32)


def gather_kernel(zs, x_ref, out_ref, send, recv):
    w = lax.axis_index("wide")
    z, x, c = w // 4, (w // 2) % 2, w % 2

    def at(zz, xx, cc):
        return (zz * 2 + xx) * 2 + cc

    peers = [at((z + d) % zs, x, c) for d in range(1, zs)] + [at(z, 1 - x, c), at(z, x, 1 - c)]
    barrier = pltpu.get_barrier_semaphore()
    for p in peers:
        pl.semaphore_signal(barrier, inc=1, device_id={"wide": p}, device_id_type=MESH)
    pl.semaphore_wait(barrier, len(peers))

    copies = []

    def put(src, slot, k, target):
        cp = pltpu.make_async_remote_copy(
            src_ref=src, dst_ref=out_ref.at[slot], send_sem=send.at[k], recv_sem=recv.at[k],
            device_id={"wide": target}, device_id_type=MESH)
        cp.start()
        copies.append(cp)
        return cp

    along_z = [put(x_ref, w, d - 1, at((z + d) % zs, x, c)) for d in range(1, zs)]
    base_x = zs - 1
    base_c = base_x + zs
    along_x = [put(x_ref, w, base_x, at(z, 1 - x, c))]
    along_c = [put(x_ref, w, base_c, at(z, x, 1 - c))]
    out_ref[w] = x_ref[...]
    for d in range(1, zs):
        along_z[d - 1].wait_recv()
        slot = at((z + zs - d) % zs, x, c)
        along_x.append(put(out_ref.at[slot], slot, base_x + d, at(z, 1 - x, c)))
        along_c.append(put(out_ref.at[slot], slot, base_c + d, at(z, x, 1 - c)))
    for d in range(zs):
        along_x[d].wait_recv()
        slot = at((z + zs - d) % zs, 1 - x, c)
        along_c.append(put(out_ref.at[slot], slot, base_c + zs + d, at(z, x, 1 - c)))
    for cp in along_c:
        cp.wait_recv()
    for cp in copies:
        cp.wait_send()


def gather_wide(block, wide, ident):
    zs = wide // 4
    n = zs - 1 + zs + 2 * zs
    vm = pl.BlockSpec(memory_space=pltpu.VMEM)
    return pl.pallas_call(
        functools.partial(gather_kernel, zs),
        out_shape=jax.ShapeDtypeStruct((wide,) + block.shape, block.dtype),
        in_specs=[vm], out_specs=vm,
        scratch_shapes=[pltpu.SemaphoreType.DMA((n,)), pltpu.SemaphoreType.DMA((n,))],
        compiler_params=pltpu.CompilerParams(collective_id=ident, has_side_effects=True),
        name=f"gather{ident}",
    )(block)


def data_kernel(zs, parts, depth, obs_ref, hess_hbm, out_ref, hess, own32, mine, rows16, spread, wide_op, part, came,
                load, send, recv, send_n, recv_n):
    w, k = lax.axis_index("wide"), lax.axis_index("narrow")
    z, x, c = w // 4, (w // 2) % 2, w % 2
    step = hess.shape[0] // parts
    blocks = mine.shape[0]

    def at(zz, xx, cc):
        return (zz * 2 + xx) * 2 + cc

    def fetch(g):
        rows = pl.ds(pl.multiple_of(g * step, 16), step)
        return pltpu.make_async_copy(hess_hbm.at[rows], hess.at[rows], load.at[g])

    for g in range(parts):
        fetch(g).start()

    peers = [at((z + d) % zs, x, c) for d in range(1, zs)] + [at(z, 1 - x, c), at(z, x, 1 - c)]
    barrier = pltpu.get_barrier_semaphore()
    for p in peers:
        pl.semaphore_signal(barrier, inc=1, device_id={"wide": p}, device_id_type=MESH)
    pl.semaphore_signal(barrier, inc=1, device_id={"narrow": 1 - k}, device_id_type=MESH)
    for b in range(blocks):
        own32[b:b + 1, :] = obs_ref[0:1, b * LANES:(b + 1) * LANES].astype(jnp.float32)
    mine[...] = own32[...].astype(jnp.bfloat16)
    pl.semaphore_wait(barrier, len(peers) + 1)

    copies = []

    def put(src, slot, n, target):
        cp = pltpu.make_async_remote_copy(
            src_ref=src, dst_ref=rows16.at[slot], send_sem=send.at[n], recv_sem=recv.at[n],
            device_id={"wide": target}, device_id_type=MESH)
        cp.start()
        copies.append(cp)
        return cp

    base_x, base_c = zs - 1, 2 * zs - 1
    along_z = [put(mine, w, d - 1, at((z + d) % zs, x, c)) for d in range(1, zs)]
    along_x = [put(mine, w, base_x, at(z, 1 - x, c))]
    along_c = [put(mine, w, base_c, at(z, x, 1 - c))]

    def place(block, slot):
        spread[pl.ds(slot, blocks, stride=4 * zs), :] = block.astype(jnp.float32)

    place(mine[...], w)
    for d in range(1, zs):
        along_z[d - 1].wait_recv()
        slot = at((z + zs - d) % zs, x, c)
        along_x.append(put(rows16.at[slot], slot, base_x + d, at(z, 1 - x, c)))
        along_c.append(put(rows16.at[slot], slot, base_c + d, at(z, x, 1 - c)))
        place(rows16[slot], slot)
    for d in range(zs):
        along_x[d].wait_recv()
        slot = at((z + zs - d) % zs, 1 - x, c)
        along_c.append(put(rows16.at[slot], slot, base_c + zs + d, at(z, x, 1 - c)))
        place(rows16[slot], slot)
    for d in range(2 * zs):
        along_c[d].wait_recv()
        slot = at((z + zs - d) % zs, x, 1 - c) if d < zs else at((z + 2 * zs - d) % zs, 1 - x, 1 - c)
        place(rows16[slot], slot)
    scen = 4 * zs
    for b in range(blocks):
        wide_op[:, b * LANES:(b + 1) * LANES] = spread[b * scen:(b + 1) * scen, :].astype(jnp.bfloat16)

    def across(g):
        return pltpu.make_async_remote_copy(
            src_ref=part.at[g], dst_ref=came.at[g], send_sem=send_n.at[g], recv_sem=recv_n.at[g],
            device_id={"narrow": 1 - k}, device_id_type=MESH)

    def product(g, _):
        fetch(g).wait()
        rows = pl.ds(pl.multiple_of(g * step, 16), step)
        total = None
        for d in range(0, wide_op.shape[1], depth):
            term = lax.dot_general(
                wide_op[:, d:d + depth], hess[rows, d:d + depth], (((1,), (1,)), ((), ())),
                preferred_element_type=jnp.float32)
            total = term if total is None else total + term
        part[g] = total

        @pl.when(g > 0)
        def _():
            across(g - 1).start()
        return 0

    lax.fori_loop(0, parts, product, 0)
    for cp in copies:
        cp.wait_send()
    across(parts - 1).start()

    def gather(g, _):
        across(g).wait()
        out_ref[g] = part[g] + came[g]
        return 0

    lax.fori_loop(0, parts, gather, 0)


def data_product(observations, hess, wide, ident):
    rows, cols = hess.shape
    zs, blocks, parts = wide // 4, cols // LANES, 7
    depth = LANES * max(d for d in range(1, 17) if blocks % d == 0)
    n = zs - 1 + zs + 2 * zs
    vm = pl.BlockSpec(memory_space=pltpu.VMEM)
    f32, bf16, dma = jnp.float32, jnp.bfloat16, pltpu.SemaphoreType.DMA
    shape = (parts, wide, rows // parts)
    got = pl.pallas_call(
        functools.partial(data_kernel, zs, parts, depth),
        out_shape=jax.ShapeDtypeStruct(shape, f32),
        in_specs=[vm, pl.BlockSpec(memory_space=pltpu.HBM)], out_specs=vm,
        scratch_shapes=[
            pltpu.VMEM((rows, cols), bf16), pltpu.VMEM((blocks, LANES), f32), pltpu.VMEM((blocks, LANES), bf16),
            pltpu.VMEM((wide, blocks, LANES), bf16), pltpu.VMEM((wide * blocks, LANES), f32),
            pltpu.VMEM((wide, cols), bf16), pltpu.VMEM(shape, f32), pltpu.VMEM(shape, f32),
            dma((parts,)), dma((n,)), dma((n,)), dma((parts,)), dma((parts,)),
        ],
        compiler_params=pltpu.CompilerParams(
            collective_id=ident, has_side_effects=True, vmem_limit_bytes=56 << 20),
        name="data",
    )(observations, hess)
    return got.transpose(1, 0, 2).reshape(wide, rows)


def map_kernel(fs, groups, half, x_ref, a_hbm, out_ref, a, m32, sent, load, send, recv):
    k = lax.axis_index("narrow")
    other = 1 - k

    def fetch(g, side, h):
        rows = pl.ds(pl.multiple_of(h * half, 64), half)
        return pltpu.make_async_copy(
            a_hbm.at[pl.ds(g * fs, fs), :, rows], a.at[pl.ds(g * fs, fs), :, rows], load.at[side, g])

    for g in range(groups):
        fetch(g, 0, other).start()
    for g in range(groups):
        fetch(g, 1, k).start()

    barrier = pltpu.get_barrier_semaphore()
    pl.semaphore_signal(barrier, inc=1, device_id={"narrow": other}, device_id_type=MESH)
    pl.semaphore_wait(barrier, 1)

    m32[...] = jnp.zeros_like(m32)
    lane = lax.broadcasted_iota(jnp.int32, (8, LANES), 1)

    def chunk(g, h, dst):
        p0 = pl.multiple_of(h * half, 64)
        for i in range(fs):
            f = g * fs + i
            parts = []
            for c in range(2):
                head = a[f, c, pl.ds(p0, 128), :]
                tail = a[f, c, pl.ds(p0 + 128, 64), :]
                parts.append(jnp.concatenate([head, tail, tail], axis=0))
            got = lax.dot_general(
                x_ref[f], jnp.concatenate(parts, axis=1), (((1,), (1,)), ((), ())),
                preferred_element_type=jnp.float32)
            for c in range(2):
                low, high = got[c * 16:c * 16 + 8], got[c * 16 + 8:c * 16 + 16]
                rows = pl.ds(c * 16 + i, 8, stride=32)
                m32[0, rows, :] = low[:, :LANES]
                m32[1, rows, :] = high[:, :LANES]
                m32[2, rows, :] = jnp.where(lane < 64, low[:, LANES:], high[:, LANES:])
        for b in range(3):
            dst[:, :, b * LANES:(b + 1) * LANES] = m32[b].reshape(8, 32, LANES).astype(jnp.bfloat16)

    def across(g):
        return pltpu.make_async_remote_copy(
            src_ref=sent.at[g], dst_ref=out_ref.at[k, g], send_sem=send.at[g], recv_sem=recv.at[g],
            device_id={"narrow": other}, device_id_type=MESH)

    def first(g, _):
        fetch(g, 0, other).wait()
        chunk(g, other, sent.at[g])

        @pl.when(g > 0)
        def _():
            across(g - 1).start()
        return 0

    lax.fori_loop(0, groups, first, 0)

    def second(g, _):
        fetch(g, 1, k).wait()
        chunk(g, k, out_ref.at[k, g])

        @pl.when(g == 0)
        def _():
            across(groups - 1).start()
        return 0

    lax.fori_loop(0, groups, second, 0)

    def drain(g, _):
        across(g).wait()
        return 0

    lax.fori_loop(0, groups, drain, 0)


def apply_maps(x, maps, fs, ident):
    nf, _, points, sensors = maps.shape
    groups, half = nf // fs, points // 2
    vm = pl.BlockSpec(memory_space=pltpu.VMEM)
    return pl.pallas_call(
        functools.partial(map_kernel, fs, groups, half),
        out_shape=jax.ShapeDtypeStruct((2, groups, 8, 32, 2 * half), jnp.bfloat16),
        in_specs=[vm, pl.BlockSpec(memory_space=pltpu.HBM)], out_specs=vm,
        scratch_shapes=[
            pltpu.VMEM(maps.shape, jnp.bfloat16),
            pltpu.VMEM((3, 8 * 32, LANES), jnp.float32),
            pltpu.VMEM((groups, 8, 32, 2 * half), jnp.bfloat16),
            pltpu.SemaphoreType.DMA((2, groups)),
            pltpu.SemaphoreType.DMA((groups,)),
            pltpu.SemaphoreType.DMA((groups,)),
        ],
        compiler_params=pltpu.CompilerParams(
            collective_id=ident, has_side_effects=True, vmem_limit_bytes=48 << 20),
        name="maps",
    )(x, maps)


def time_kernel(scale, m_ref, hi_ref, lo_ref, out_ref):
    blocks, nt = m_ref.shape[0], out_ref.shape[2]
    for j in range(8):
        m = m_ref[:, j].reshape(blocks * 32, m_ref.shape[3])
        got = lax.dot_general(m, hi_ref[...], (((0,), (0,)), ((), ())), preferred_element_type=jnp.float32)
        got += lax.dot_general(m, lo_ref[...], (((0,), (0,)), ((), ())), preferred_element_type=jnp.float32)
        got = (got * scale)[:, :nt]
        out_ref[0:128, j, :] = got[0:128]
        out_ref[0:128, j + 8, :] = got[128:256]
        out_ref[128:192, j, :] = got[256:320]
        out_ref[128:192, j + 8, :] = got[320:384]


def to_time(m, nt, nf, fs):
    blocks = m.shape[0] * m.shape[1]
    table = synthesis_table(nt, nf)
    laid = np.zeros((blocks, 2, 16, 256), np.float32)
    laid[:, :, :fs, :nt] = table.reshape(blocks, fs, 2, nt).transpose(0, 2, 1, 3)
    laid = laid.reshape(blocks * 32, 256)
    hi = laid.astype(jnp.bfloat16)
    lo = (laid - hi.astype(np.float32)).astype(jnp.bfloat16)
    vm = pl.BlockSpec(memory_space=pltpu.VMEM)
    return pl.pallas_call(
        functools.partial(time_kernel, 1.0 / nf),
        out_shape=jax.ShapeDtypeStruct((m.shape[4] // 2, 16, nt), jnp.float32),
        in_specs=[vm] * 3, out_specs=vm,
        compiler_params=pltpu.CompilerParams(vmem_limit_bytes=32 << 20),
        name="time",
    )(m.reshape((blocks,) + m.shape[2:]), jnp.asarray(hi), jnp.asarray(lo))


def per_device(wide, narrow, hess_inverse, observations, adjoint_maps):
    highest = lax.Precision.HIGHEST
    nf_dev, _, points, sensors = adjoint_maps.shape
    nf = nf_dev * narrow
    rows, cols = hess_inverse.shape
    nt = rows * wide // sensors
    scen = observations.shape[0] * wide
    sensors_dev = rows // nt
    fs = max([d for d in range(1, 17) if nf_dev % d == 0])
    tuned = (narrow == 2 and wide == 16 and scen == 16 and sensors == 128 and points == 384
             and cols % LANES == 0 and observations.shape[0] == 1 and rows % 112 == 0)
    table = jnp.asarray(analysis_table(nt, nf))
    if not tuned:
        observed = lax.all_gather(observations, "wide", axis=0, tiled=True)
        values = lax.dot_general(
            observed, hess_inverse, (((1,), (1,)), ((), ())), preferred_element_type=jnp.float32)
        values = values.reshape(scen, sensors_dev, nt)
        terms = jnp.einsum("nst,tcf->sfcn", values, table, precision=highest)
        spectra = lax.psum_scatter(terms, "narrow", scatter_dimension=1, tiled=True).astype(jnp.bfloat16)
        portion = lax.all_gather(spectra, "wide", axis=0, tiled=True)
        both = portion.transpose(1, 2, 3, 0)
        re, im = both[:, 0], both[:, 1]
        x = jnp.concatenate([jnp.concatenate([re, -im], 2), jnp.concatenate([im, re], 2)], 1)
        a = adjoint_maps.transpose(0, 2, 1, 3).reshape(nf_dev, points, 2 * sensors)
        m = jnp.einsum("frk,fpk->frp", x, a, preferred_element_type=jnp.float32).astype(jnp.bfloat16)
        m = m.reshape(nf_dev, 2, scen, points)
        m = lax.all_to_all(m, "narrow", split_axis=3, concat_axis=0, tiled=True)
        est = jnp.einsum("fcnp,fct->ptn", m.astype(jnp.float32), jnp.asarray(synthesis_table(nt, nf)),
                         precision=highest)
        return est * (1.0 / nf)
    values = data_product(observations, hess_inverse, wide, 0).reshape(scen, sensors_dev, nt)
    mine = lax.dynamic_slice_in_dim(table, lax.axis_index("narrow") * nf_dev, nf_dev, 2)
    spectra = jnp.einsum("nst,tcf->scnf", values, mine, precision=highest)
    spectra = spectra.reshape(-1, nf_dev).astype(jnp.bfloat16)
    full = gather_wide(spectra, wide, 1).reshape(sensors, 2, scen, nf_dev)
    both = full.transpose(3, 1, 2, 0)
    re, im = both[:, 0], both[:, 1]
    x = jnp.concatenate([jnp.concatenate([re, -im], 2), jnp.concatenate([im, re], 2)], 1)
    m = apply_maps(x, adjoint_maps, fs, 2)
    return to_time(m, nt, nf, fs).transpose(0, 2, 1)


def solution(mesh):
    wide, narrow = mesh.shape["wide"], mesh.shape["narrow"]
    return jax.shard_map(
        functools.partial(per_device, wide, narrow),
        mesh=mesh,
        in_specs=(P("wide", "narrow"), P("wide", "narrow"), P("narrow", None, "wide", None)),
        out_specs=P(("wide", "narrow"), None, None),
        check_vma=False,
    )
```

```python
import functools
import math

import jax
import jax.numpy as jnp
import numpy as np
from jax import lax
from jax.experimental import pallas as pl
from jax.experimental.pallas import tpu as pltpu
from jax.sharding import PartitionSpec as P

MESH = pl.DeviceIdType.MESH
LANES = 128


def angles(freqs, times, turn):
    return 2.0 * math.pi * ((freqs * times) % turn) / turn


def analysis_table(nt, nf):
    a = angles(np.arange(nt)[:, None], np.arange(nf)[None, :], 2 * nf)
    return np.stack([np.cos(a), -np.sin(a)], axis=1).astype(np.float32)


def synthesis_table(nt, nf):
    a = angles(np.arange(nf)[:, None], np.arange(nt)[None, :], 2 * nf)
    return np.stack([np.cos(a), -np.sin(a)], axis=1).astype(np.float32)


def gather_kernel(zs, x_ref, out_ref, send, recv):
    w = lax.axis_index("wide")
    z, x, c = w // 4, (w // 2) % 2, w % 2

    def at(zz, xx, cc):
        return (zz * 2 + xx) * 2 + cc

    peers = [at((z + d) % zs, x, c) for d in range(1, zs)] + [at(z, 1 - x, c), at(z, x, 1 - c)]
    barrier = pltpu.get_barrier_semaphore()
    for p in peers:
        pl.semaphore_signal(barrier, inc=1, device_id={"wide": p}, device_id_type=MESH)
    pl.semaphore_wait(barrier, len(peers))

    copies = []

    def put(src, slot, k, target):
        cp = pltpu.make_async_remote_copy(
            src_ref=src, dst_ref=out_ref.at[slot], send_sem=send.at[k], recv_sem=recv.at[k],
            device_id={"wide": target}, device_id_type=MESH)
        cp.start()
        copies.append(cp)
        return cp

    along_z = [put(x_ref, w, d - 1, at((z + d) % zs, x, c)) for d in range(1, zs)]
    base_x = zs - 1
    base_c = base_x + zs
    along_x = [put(x_ref, w, base_x, at(z, 1 - x, c))]
    along_c = [put(x_ref, w, base_c, at(z, x, 1 - c))]
    out_ref[w] = x_ref[...]
    for d in range(1, zs):
        along_z[d - 1].wait_recv()
        slot = at((z + zs - d) % zs, x, c)
        along_x.append(put(out_ref.at[slot], slot, base_x + d, at(z, 1 - x, c)))
        along_c.append(put(out_ref.at[slot], slot, base_c + d, at(z, x, 1 - c)))
    for d in range(zs):
        along_x[d].wait_recv()
        slot = at((z + zs - d) % zs, 1 - x, c)
        along_c.append(put(out_ref.at[slot], slot, base_c + zs + d, at(z, x, 1 - c)))
    for cp in along_c:
        cp.wait_recv()
    for cp in copies:
        cp.wait_send()


def gather_wide(block, wide, ident):
    zs = wide // 4
    n = zs - 1 + zs + 2 * zs
    vm = pl.BlockSpec(memory_space=pltpu.VMEM)
    return pl.pallas_call(
        functools.partial(gather_kernel, zs),
        out_shape=jax.ShapeDtypeStruct((wide,) + block.shape, block.dtype),
        in_specs=[vm], out_specs=vm,
        scratch_shapes=[pltpu.SemaphoreType.DMA((n,)), pltpu.SemaphoreType.DMA((n,))],
        compiler_params=pltpu.CompilerParams(collective_id=ident, has_side_effects=True),
        name=f"gather{ident}",
    )(block)


def data_kernel(zs, parts, depth, obs_ref, hess_hbm, out_ref, hess, own32, mine, rows16, spread, wide_op, part, came,
                load, send, recv, send_n, recv_n):
    w, k = lax.axis_index("wide"), lax.axis_index("narrow")
    z, x, c = w // 4, (w // 2) % 2, w % 2
    step = hess.shape[0] // parts
    blocks = mine.shape[0]

    def at(zz, xx, cc):
        return (zz * 2 + xx) * 2 + cc

    def fetch(g):
        rows = pl.ds(pl.multiple_of(g * step, 16), step)
        return pltpu.make_async_copy(hess_hbm.at[rows], hess.at[rows], load.at[g])

    for g in range(parts):
        fetch(g).start()

    peers = [at((z + d) % zs, x, c) for d in range(1, zs)] + [at(z, 1 - x, c), at(z, x, 1 - c)]
    barrier = pltpu.get_barrier_semaphore()
    for p in peers:
        pl.semaphore_signal(barrier, inc=1, device_id={"wide": p}, device_id_type=MESH)
    pl.semaphore_signal(barrier, inc=1, device_id={"narrow": 1 - k}, device_id_type=MESH)
    for b in range(blocks):
        own32[b:b + 1, :] = obs_ref[0:1, b * LANES:(b + 1) * LANES].astype(jnp.float32)
    mine[...] = own32[...].astype(jnp.bfloat16)
    pl.semaphore_wait(barrier, len(peers) + 1)

    copies = []

    def put(src, slot, n, target):
        cp = pltpu.make_async_remote_copy(
            src_ref=src, dst_ref=rows16.at[slot], send_sem=send.at[n], recv_sem=recv.at[n],
            device_id={"wide": target}, device_id_type=MESH)
        cp.start()
        copies.append(cp)
        return cp

    base_x, base_c = zs - 1, 2 * zs - 1
    along_z = [put(mine, w, d - 1, at((z + d) % zs, x, c)) for d in range(1, zs)]
    along_x = [put(mine, w, base_x, at(z, 1 - x, c))]
    along_c = [put(mine, w, base_c, at(z, x, 1 - c))]

    def place(block, slot):
        spread[pl.ds(slot, blocks, stride=4 * zs), :] = block.astype(jnp.float32)

    place(mine[...], w)
    for d in range(1, zs):
        along_z[d - 1].wait_recv()
        slot = at((z + zs - d) % zs, x, c)
        along_x.append(put(rows16.at[slot], slot, base_x + d, at(z, 1 - x, c)))
        along_c.append(put(rows16.at[slot], slot, base_c + d, at(z, x, 1 - c)))
        place(rows16[slot], slot)
    for d in range(zs):
        along_x[d].wait_recv()
        slot = at((z + zs - d) % zs, 1 - x, c)
        along_c.append(put(rows16.at[slot], slot, base_c + zs + d, at(z, x, 1 - c)))
        place(rows16[slot], slot)
    for d in range(2 * zs):
        along_c[d].wait_recv()
        slot = at((z + zs - d) % zs, x, 1 - c) if d < zs else at((z + 2 * zs - d) % zs, 1 - x, 1 - c)
        place(rows16[slot], slot)
    scen = 4 * zs
    for b in range(blocks):
        wide_op[:, b * LANES:(b + 1) * LANES] = spread[b * scen:(b + 1) * scen, :].astype(jnp.bfloat16)

    def across(g):
        return pltpu.make_async_remote_copy(
            src_ref=part.at[g], dst_ref=came.at[g], send_sem=send_n.at[g], recv_sem=recv_n.at[g],
            device_id={"narrow": 1 - k}, device_id_type=MESH)

    def product(g, _):
        fetch(g).wait()
        rows = pl.ds(pl.multiple_of(g * step, 16), step)
        total = None
        for d in range(0, wide_op.shape[1], depth):
            term = lax.dot_general(
                wide_op[:, d:d + depth], hess[rows, d:d + depth], (((1,), (1,)), ((), ())),
                preferred_element_type=jnp.float32)
            total = term if total is None else total + term
        part[g] = total

        @pl.when(g > 0)
        def _():
            across(g - 1).start()
        return 0

    lax.fori_loop(0, parts, product, 0)
    for cp in copies:
        cp.wait_send()
    across(parts - 1).start()

    def gather(g, _):
        across(g).wait()
        out_ref[g] = part[g] + came[g]
        return 0

    lax.fori_loop(0, parts, gather, 0)


def data_product(observations, hess, wide, ident):
    rows, cols = hess.shape
    zs, blocks, parts = wide // 4, cols // LANES, 7
    depth = LANES * max(d for d in range(1, 17) if blocks % d == 0)
    n = zs - 1 + zs + 2 * zs
    vm = pl.BlockSpec(memory_space=pltpu.VMEM)
    f32, bf16, dma = jnp.float32, jnp.bfloat16, pltpu.SemaphoreType.DMA
    shape = (parts, wide, rows // parts)
    got = pl.pallas_call(
        functools.partial(data_kernel, zs, parts, depth),
        out_shape=jax.ShapeDtypeStruct(shape, f32),
        in_specs=[vm, pl.BlockSpec(memory_space=pltpu.HBM)], out_specs=vm,
        scratch_shapes=[
            pltpu.VMEM((rows, cols), bf16), pltpu.VMEM((blocks, LANES), f32), pltpu.VMEM((blocks, LANES), bf16),
            pltpu.VMEM((wide, blocks, LANES), bf16), pltpu.VMEM((wide * blocks, LANES), f32),
            pltpu.VMEM((wide, cols), bf16), pltpu.VMEM(shape, f32), pltpu.VMEM(shape, f32),
            dma((parts,)), dma((n,)), dma((n,)), dma((parts,)), dma((parts,)),
        ],
        compiler_params=pltpu.CompilerParams(
            collective_id=ident, has_side_effects=True, vmem_limit_bytes=56 << 20),
        name="data",
    )(observations, hess)
    return got.transpose(1, 0, 2).reshape(wide, rows)


def map_kernel(fs, groups, half, x_ref, a_hbm, out_ref, a, m32, sent, load, send, recv):
    k = lax.axis_index("narrow")
    other = 1 - k

    def fetch(g, side, h):
        rows = pl.ds(pl.multiple_of(h * half, 64), half)
        return pltpu.make_async_copy(
            a_hbm.at[pl.ds(g * fs, fs), :, rows], a.at[pl.ds(g * fs, fs), :, rows], load.at[side, g])

    for g in range(groups):
        fetch(g, 0, other).start()
    for g in range(groups):
        fetch(g, 1, k).start()

    barrier = pltpu.get_barrier_semaphore()
    pl.semaphore_signal(barrier, inc=1, device_id={"narrow": other}, device_id_type=MESH)
    pl.semaphore_wait(barrier, 1)

    m32[...] = jnp.zeros_like(m32)
    lane = lax.broadcasted_iota(jnp.int32, (8, LANES), 1)

    def chunk(g, h, dst):
        p0 = pl.multiple_of(h * half, 64)
        for i in range(fs):
            f = g * fs + i
            parts = []
            for c in range(2):
                head = a[f, c, pl.ds(p0, 128), :]
                tail = a[f, c, pl.ds(p0 + 128, 64), :]
                parts.append(jnp.concatenate([head, tail, tail], axis=0))
            got = lax.dot_general(
                x_ref[f], jnp.concatenate(parts, axis=1), (((1,), (1,)), ((), ())),
                preferred_element_type=jnp.float32)
            for c in range(2):
                low, high = got[c * 16:c * 16 + 8], got[c * 16 + 8:c * 16 + 16]
                rows = pl.ds(c * 16 + i, 8, stride=32)
                m32[0, rows, :] = low[:, :LANES]
                m32[1, rows, :] = high[:, :LANES]
                m32[2, rows, :] = jnp.where(lane < 64, low[:, LANES:], high[:, LANES:])
        for b in range(3):
            dst[:, :, b * LANES:(b + 1) * LANES] = m32[b].reshape(8, 32, LANES).astype(jnp.bfloat16)

    def across(g):
        return pltpu.make_async_remote_copy(
            src_ref=sent.at[g], dst_ref=out_ref.at[k, g], send_sem=send.at[g], recv_sem=recv.at[g],
            device_id={"narrow": other}, device_id_type=MESH)

    def first(g, _):
        fetch(g, 0, other).wait()
        chunk(g, other, sent.at[g])

        @pl.when(g > 0)
        def _():
            across(g - 1).start()
        return 0

    lax.fori_loop(0, groups, first, 0)

    def second(g, _):
        fetch(g, 1, k).wait()
        chunk(g, k, out_ref.at[k, g])

        @pl.when(g == 0)
        def _():
            across(groups - 1).start()
        return 0

    lax.fori_loop(0, groups, second, 0)

    def drain(g, _):
        across(g).wait()
        return 0

    lax.fori_loop(0, groups, drain, 0)


def apply_maps(x, maps, fs, ident):
    nf, _, points, sensors = maps.shape
    groups, half = nf // fs, points // 2
    vm = pl.BlockSpec(memory_space=pltpu.VMEM)
    return pl.pallas_call(
        functools.partial(map_kernel, fs, groups, half),
        out_shape=jax.ShapeDtypeStruct((2, groups, 8, 32, 2 * half), jnp.bfloat16),
        in_specs=[vm, pl.BlockSpec(memory_space=pltpu.HBM)], out_specs=vm,
        scratch_shapes=[
            pltpu.VMEM(maps.shape, jnp.bfloat16),
            pltpu.VMEM((3, 8 * 32, LANES), jnp.float32),
            pltpu.VMEM((groups, 8, 32, 2 * half), jnp.bfloat16),
            pltpu.SemaphoreType.DMA((2, groups)),
            pltpu.SemaphoreType.DMA((groups,)),
            pltpu.SemaphoreType.DMA((groups,)),
        ],
        compiler_params=pltpu.CompilerParams(
            collective_id=ident, has_side_effects=True, vmem_limit_bytes=48 << 20),
        name="maps",
    )(x, maps)


def time_kernel(scale, m_ref, table_ref, out_hbm, laid, sem):
    blocks, nt = m_ref.shape[0], laid.shape[2]

    def back(j, lanes):
        m = m_ref[:, j, :, lanes].reshape(blocks * 32, lanes.stop - lanes.start)
        got = lax.dot_general(m, table_ref[...], (((0,), (0,)), ((), ())), preferred_element_type=jnp.float32)
        return (got * scale)[:, :nt]

    def leave(n, rows):
        return pltpu.make_async_copy(laid.at[rows], out_hbm.at[rows], sem.at[n])

    first, second = leave(0, pl.ds(0, 128)), leave(1, pl.ds(128, 64))
    for j in range(8):
        got = back(j, slice(0, 256))
        laid[0:128, j, :] = got[0:128]
        laid[0:128, j + 8, :] = got[128:256]
    first.start()
    for j in range(8):
        got = back(j, slice(256, 384))
        laid[128:192, j, :] = got[0:64]
        laid[128:192, j + 8, :] = got[64:128]
    second.start()
    first.wait()
    second.wait()


def to_time(m, nt, nf, fs):
    blocks = m.shape[0] * m.shape[1]
    table = synthesis_table(nt, nf)
    laid = np.zeros((blocks, 2, 16, 256), np.float32)
    laid[:, :, :fs, :nt] = table.reshape(blocks, fs, 2, nt).transpose(0, 2, 1, 3)
    laid = laid.reshape(blocks * 32, 256)
    laid = laid.astype(jnp.bfloat16)
    vm = pl.BlockSpec(memory_space=pltpu.VMEM)
    return pl.pallas_call(
        functools.partial(time_kernel, 1.0 / nf),
        out_shape=jax.ShapeDtypeStruct((m.shape[4] // 2, 16, nt), jnp.float32),
        in_specs=[vm] * 2, out_specs=pl.BlockSpec(memory_space=pltpu.HBM),
        scratch_shapes=[pltpu.VMEM((m.shape[4] // 2, 16, nt), jnp.float32), pltpu.SemaphoreType.DMA((2,))],
        compiler_params=pltpu.CompilerParams(vmem_limit_bytes=32 << 20),
        name="time",
    )(m.reshape((blocks,) + m.shape[2:]), jnp.asarray(laid))


def per_device(wide, narrow, hess_inverse, observations, adjoint_maps):
    highest = lax.Precision.HIGHEST
    nf_dev, _, points, sensors = adjoint_maps.shape
    nf = nf_dev * narrow
    rows, cols = hess_inverse.shape
    nt = rows * wide // sensors
    scen = observations.shape[0] * wide
    sensors_dev = rows // nt
    fs = max([d for d in range(1, 17) if nf_dev % d == 0])
    tuned = (narrow == 2 and wide == 16 and scen == 16 and sensors == 128 and points == 384
             and cols % LANES == 0 and observations.shape[0] == 1 and rows % 112 == 0)
    table = jnp.asarray(analysis_table(nt, nf))
    if not tuned:
        observed = lax.all_gather(observations, "wide", axis=0, tiled=True)
        values = lax.dot_general(
            observed, hess_inverse, (((1,), (1,)), ((), ())), preferred_element_type=jnp.float32)
        values = values.reshape(scen, sensors_dev, nt)
        terms = jnp.einsum("nst,tcf->sfcn", values, table, precision=highest)
        spectra = lax.psum_scatter(terms, "narrow", scatter_dimension=1, tiled=True).astype(jnp.bfloat16)
        portion = lax.all_gather(spectra, "wide", axis=0, tiled=True)
        both = portion.transpose(1, 2, 3, 0)
        re, im = both[:, 0], both[:, 1]
        x = jnp.concatenate([jnp.concatenate([re, -im], 2), jnp.concatenate([im, re], 2)], 1)
        a = adjoint_maps.transpose(0, 2, 1, 3).reshape(nf_dev, points, 2 * sensors)
        m = jnp.einsum("frk,fpk->frp", x, a, preferred_element_type=jnp.float32).astype(jnp.bfloat16)
        m = m.reshape(nf_dev, 2, scen, points)
        m = lax.all_to_all(m, "narrow", split_axis=3, concat_axis=0, tiled=True)
        est = jnp.einsum("fcnp,fct->ptn", m.astype(jnp.float32), jnp.asarray(synthesis_table(nt, nf)),
                         precision=highest)
        return est * (1.0 / nf)
    values = data_product(observations, hess_inverse, wide, 0).reshape(scen, sensors_dev, nt)
    mine = lax.dynamic_slice_in_dim(table, lax.axis_index("narrow") * nf_dev, nf_dev, 2)
    spectra = jnp.einsum("nst,tcf->scnf", values, mine, precision=highest)
    spectra = spectra.reshape(-1, nf_dev).astype(jnp.bfloat16)
    full = gather_wide(spectra, wide, 1).reshape(sensors, 2, scen, nf_dev)
    both = full.transpose(3, 1, 2, 0)
    re, im = both[:, 0], both[:, 1]
    x = jnp.concatenate([jnp.concatenate([re, -im], 2), jnp.concatenate([im, re], 2)], 1)
    m = apply_maps(x, adjoint_maps, fs, 2)
    return to_time(m, nt, nf, fs).transpose(0, 2, 1)


def solution(mesh):
    wide, narrow = mesh.shape["wide"], mesh.shape["narrow"]
    return jax.shard_map(
        functools.partial(per_device, wide, narrow),
        mesh=mesh,
        in_specs=(P("wide", "narrow"), P("wide", "narrow"), P("narrow", None, "wide", None)),
        out_specs=P(("wide", "narrow"), None, None),
        check_vma=False,
    )
```
